32 devices in a mesh: leaf: 8 (over z, y), sub: 4 (over x, core).
Axes of the slice: x: 2, y: 2, z: 4, core: 2. Of those that a mesh axis runs over, the one named last changes fastest.
Arguments:
- points: float32 [3, 32768], P(None, ('leaf', 'sub')), may hold values from 0 to 4
- order: int32 [32, 1024], P(('leaf', 'sub')), may hold values from 0 to 1023, each once within a row
- counts: int32 [32], P(('leaf', 'sub')), may hold values from 1 to 1024, 24576 in all
- basis: float32 [32768, 640], P(('leaf', 'sub')), may hold values from -0.1875 to 0.1875
- right_side: float32 [32768, 128], P(('leaf', 'sub')), may hold values from -6 to 6
- coupling: float32 [5, 256, 256], replicated, may hold values from -0.375 to 0.375
Outputs:
- solution: float32 [32768, 128], P(('leaf', 'sub'))
The draws below stay inside these ranges and needn't reach their ends.
Inputs may be any that keep to these rules, and one draw needn't show every extreme that they name: `order`: each row orders the 1024 slots of one leaf, every slot once. `counts`: slots of a leaf at or past its count are padding; some leaf is full.
All inputs are finite; a program needn't handle non-finite values. No bound on the sum of `counts` on one device may be relied on, other than what follows from the above.
Results may differ from the reference program's by a relative error of at most 0.0003.
Values sent between devices are 32-bit elements; how exact they have to be, the bound alone decides.
No kernel may reach another device: no remote copies, remote signals or barrier semaphores. Data moves between devices by JAX's collectives and lax.ppermute only.
A program may use at most 128 MiB of HBM per device.

```python
import math
import jax
import jax.numpy as jnp
import numpy as np
from jax import lax

R = 128
NRHS = 128
LEAF = 1024
LEAVES = 32
TOTAL = 32768
LEVELS = 5
COLS = 768


def level_of(own_key, extent, pieces, low, largest):
    factor_of = 1.0
    for position, shards_of in pieces:
        draws = jax.random.uniform(jax.random.fold_in(jax.random.fold_in(own_key, 6), position), (shards_of,), jnp.float32, low / len(pieces), largest / len(pieces))
        factor_of = factor_of * jnp.repeat(jnp.exp(draws), extent[position] // shards_of).reshape((-1,) + (1,) * (len(extent) - 1 - position))
    return factor_of


def length_profile(count, total, most, skew):
    portions = [(1 << 20) // math.isqrt(grade ** skew) + 1 for grade in range(2, count + 1)]
    spare, given = total - most - (count - 1), [1] * (count - 1)
    while spare > 0:
        movable = [i for i in range(count - 1) if given[i] < most]
        mass, left = sum([portions[i] for i in movable]), spare
        for i in movable:
            extra = min(most - given[i], max(1, left * portions[i] // mass), spare)
            given[i] = given[i] + extra
            spare = spare - extra
    return np.array([most] + given)


def ragged(stream_key, number_of, total, most, slope):
    if number_of == 2:
        one = jax.random.randint(stream_key, (), max(1, total - most), min(most, total - 1) + 1)
        return jnp.stack([one, total - one])
    tallies = jnp.asarray(length_profile(number_of, total, most, slope), jnp.int32)
    twos = (number_of - 1) // 2
    source_of, taker = tallies[1:1 + 2 * twos:2], tallies[2:2 + 2 * twos:2]
    margin = jnp.minimum(source_of - 1, most - taker)
    moved = jax.random.randint(jax.random.fold_in(stream_key, 1), (twos,), 0, 1 << 20) % (margin + 1)
    tallies = tallies.at[1:1 + 2 * twos:2].set(source_of - moved).at[2:2 + 2 * twos:2].set(taker + moved)
    return tallies[jax.random.permutation(jax.random.fold_in(stream_key, 2), number_of)]


def centred(key, extent, spread, most, split=(), kind=jnp.bfloat16):
    result = jax.random.normal(key, extent, jnp.float32) * spread
    if len(split) > 0:
        result = level_of(key, extent, split, -0.22, 0.18) * result
    return jnp.clip(result, min=-most, max=most).astype(kind)


def setup_inputs(seed: int = 0) -> dict:
    seeds = jax.random.split(jax.random.key(seed), 7)
    points = jnp.clip(4.0 * jax.random.uniform(seeds[0], (3, TOTAL), jnp.float32) ** level_of(seeds[0], (3, TOTAL), ((1, 32),), -0.2, 0.2), 0.0, 4.0)
    order = jax.vmap(lambda own: jax.random.permutation(own, LEAF))(jax.random.split(seeds[1], LEAVES)).reshape((LEAVES, LEAF)).astype(jnp.int32)
    counts = ragged(seeds[2], LEAVES, 3 * LEAVES * LEAF // 4, LEAF, 1).astype(jnp.int32)
    basis = centred(seeds[3], (TOTAL, LEVELS * R), LEAF ** -0.5, 0.1875, ((0, 32),), jnp.float32)
    right_side = centred(seeds[4], (TOTAL, NRHS), 1.0, 6.0, ((0, 32),), jnp.float32)
    coupling = centred(seeds[5], (LEVELS, 2 * R, 2 * R), (2 * R) ** -0.5, 0.375, (), jnp.float32)
    return {"points": points, "order": order, "counts": counts, "basis": basis, "right_side": right_side, "coupling": coupling}


GAMMA_RATE = 2.0
NUGGET_VALUE = 1.0

def leaf_solve(packed):
    coords, ordering, count, basis_rows, rhs_rows = packed
    ordered = coords[:, ordering]
    live_mask = (jnp.arange(coords.shape[1]) < count).astype(jnp.float32)
    offsets = ordered[:, :, None] - ordered[:, None, :]
    distance = jnp.sum(offsets * offsets, axis=0)
    kernel = jnp.exp(-GAMMA_RATE * distance) * live_mask[:, None] * live_mask[None, :]
    kernel = kernel + NUGGET_VALUE * jnp.eye(coords.shape[1], dtype=jnp.float32)
    lower_tri = jnp.linalg.cholesky(kernel)
    stacked = jnp.concatenate([basis_rows, rhs_rows], axis=1) * live_mask[:, None]
    solved = jax.scipy.linalg.cho_solve((lower_tri, True), stacked)
    return (solved, stacked[:, :basis_rows.shape[1]])

def couple(first_sums, second_sums, factor):
    upper_half = factor[:R]
    lower_half = factor[R:]
    highest = lax.Precision.HIGHEST
    first_block = first_sums[:, :R]
    second_block = second_sums[:, :R]
    coupled = jnp.eye(2 * R, dtype=jnp.float32)
    coupled = coupled + jnp.dot(upper_half.T, jnp.dot(first_block, upper_half, precision=highest), precision=highest)
    coupled = coupled + jnp.dot(lower_half.T, jnp.dot(second_block, lower_half, precision=highest), precision=highest)
    coupled = 0.5 * (coupled + coupled.T)
    forcing = jnp.dot(upper_half.T, first_sums, precision=highest) + jnp.dot(lower_half.T, second_sums, precision=highest)
    lower_tri = jnp.linalg.cholesky(coupled)
    solved_coef = jax.scipy.linalg.cho_solve((lower_tri, True), forcing)
    return jnp.dot(factor, solved_coef, precision=highest)

def reference(points, order, counts, basis, right_side, coupling):
    highest = lax.Precision.HIGHEST
    coords = points.reshape(3, LEAVES, LEAF).transpose(1, 0, 2)
    solved, masked = lax.map(leaf_solve, (coords, order, counts, basis.reshape(LEAVES, LEAF, LEVELS * R), right_side.reshape(LEAVES, LEAF, NRHS)))
    for tree_level in range(LEVELS):
        col_start = tree_level * R
        span_cols = COLS - col_start
        group_size = 2 ** tree_level
        block_rows = masked[:, :, col_start:col_start + R]
        projected = jnp.einsum('gnr,gnc->grc', block_rows, solved[:, :, col_start:], precision=highest)
        child_sums = projected.reshape(LEAVES // group_size, group_size, R, span_cols).sum(axis=1)
        paired = child_sums.reshape(LEAVES // (2 * group_size), 2, R, span_cols)
        mixed = jax.vmap(couple, in_axes=(0, 0, None))(paired[:, 0], paired[:, 1], coupling[tree_level])
        per_child = mixed.reshape(LEAVES // group_size, R, span_cols)
        per_leaf = jnp.repeat(per_child, group_size, axis=0)
        basis_part = solved[:, :, col_start:col_start + R]
        update = jnp.einsum('gnr,grc->gnc', basis_part, per_leaf, precision=highest)
        solved = solved.at[:, :, col_start:].add(-update)
    return solved[:, :, LEVELS * R:].reshape(TOTAL, NRHS)
```

```python
import functools
import math

import jax
import jax.numpy as jnp
from jax import lax
from jax.experimental import pallas as pl
from jax.experimental.pallas import tpu as pltpu
from jax.sharding import PartitionSpec as P

R = 128
GAMMA_RATE = 2.0
NUGGET_VALUE = 1.0
HIGH = lax.Precision.HIGH
HIGHEST = lax.Precision.HIGHEST


def nn(a, b, precision=HIGH):
    return lax.dot_general(
        a, b, (((1,), (0,)), ((), ())), precision=precision, preferred_element_type=jnp.float32
    )


def nt(a, b, precision=HIGH):
    return lax.dot_general(
        a, b, (((1,), (1,)), ((), ())), precision=precision, preferred_element_type=jnp.float32
    )


def identity(size):
    row = lax.broadcasted_iota(jnp.int32, (size, size), 0)
    col = lax.broadcasted_iota(jnp.int32, (size, size), 1)
    return (row == col).astype(jnp.float32)


def inverse(matrix, refine):
    size = matrix.shape[0]
    eye = identity(size)
    low = 1.0 / jnp.max(jnp.sum(jnp.abs(matrix), axis=0))

    def step(carry):
        low, x, z = carry
        scale = 4.0 / ((1.0 + low) * (1.0 + low))
        shift = 1.0 + low
        return (
            low * scale,
            scale * (shift * x - nn(x, z)),
            scale * (shift * z - nn(z, z)),
        )

    _, x, _ = lax.while_loop(
        lambda carry: carry[0] < 1.0 - 6e-7, step, (low, eye * low, matrix * low)
    )
    if refine:
        x = x + nn(x, eye - nn(matrix, x, HIGHEST))
    return x


def leaf_kernel(
    count_ref, points_ref, order_ref, basis_ref, rhs_ref,
    head_ref, rest_ref, factor_ref, rows_ref, coords_ref, weighted_ref,
):
    slots = points_ref.shape[1]
    levels = basis_ref.shape[1] // R
    blocks = levels + 1
    tile = min(256, slots)
    count = count_ref[0]
    coords_ref[...] = jnp.zeros_like(coords_ref)
    coords_ref[0:3, :] = points_ref[...]
    coords = coords_ref[...]
    first = coords.astype(jnp.bfloat16).astype(jnp.float32)
    second = (coords - first).astype(jnp.bfloat16).astype(jnp.float32)
    third = coords - first - second
    parts = jnp.concatenate([first, second, third], axis=0).astype(jnp.bfloat16)
    source = lax.broadcasted_iota(jnp.int32, (slots, slots), 0)
    chosen = jnp.where(source == order_ref[...], 1.0, 0.0).astype(jnp.bfloat16)
    moved = jnp.dot(parts, chosen, preferred_element_type=jnp.float32)
    across = moved[0:8] + moved[8:16] + moved[16:24]
    down = across.T
    live_across = (lax.broadcasted_iota(jnp.int32, (1, slots), 1) < count).astype(jnp.float32)
    live_down = (lax.broadcasted_iota(jnp.int32, (slots, 1), 0) < count).astype(jnp.float32)
    for block in range(blocks):
        if block < levels:
            piece = basis_ref[:, block * R : (block + 1) * R]
        else:
            piece = rhs_ref[...]
        rows_ref[block * R : (block + 1) * R, :] = piece.T * live_across
    steps = slots // tile
    for j in range(steps):
        js = slice(j * tile, (j + 1) * tile)
        for i in range(j, steps):
            rs = slice(i * tile, (i + 1) * tile)
            total = None
            for axis in range(3):
                offset = down[rs, axis : axis + 1] - across[axis : axis + 1, js]
                square = offset * offset
                total = square if total is None else total + square
            value = jnp.exp2(total * (-GAMMA_RATE * math.log2(math.e)))
            value = value * live_down[rs] * live_across[:, js]
            if i == j:
                value = value + NUGGET_VALUE * identity(tile)
            factor_ref[rs, js] = value
    for k in range(steps):
        ks = slice(k * tile, (k + 1) * tile)
        x = inverse(factor_ref[ks, ks], False)
        factor_ref[ks, ks] = x
        own = rows_ref[:, ks]
        if k < steps - 1:
            panel = factor_ref[(k + 1) * tile :, ks]
            lower = nn(panel, x)
            factor_ref[(k + 1) * tile :, ks] = lower
            for j in range(k + 1, steps):
                js = slice(j * tile, (j + 1) * tile)
                at = (j - k - 1) * tile
                factor_ref[j * tile :, js] -= nt(lower[at:], panel[at : at + tile])
            rows_ref[:, (k + 1) * tile :] -= nt(own, lower)
        weighted_ref[:, ks] = nn(own, x)
    at = -R
    for m in range(levels):
        column = nt(weighted_ref[m * R :, :], rows_ref[m * R : (m + 1) * R, :])
        if m == 0:
            head_ref[...] = column[:R]
            rest_ref[0 : levels * R, :] = column[R:]
        else:
            rest_ref[at : at + (blocks - m) * R, :] = column
        at += (blocks - m) * R


def packed_rows(levels, level):
    return sum(levels + 1 - m for m in range(level, levels)) * R - R


def invert_kernel(side_ref, own_ref, sibling_ref, factor_ref, inverse_ref):
    side = side_ref[0]
    mine = factor_ref[0, pl.ds(pl.multiple_of(side * R, R), R), :]
    theirs = factor_ref[0, pl.ds(pl.multiple_of((1 - side) * R, R), R), :]
    pair = jnp.concatenate([mine, theirs], axis=0)
    inner = jnp.concatenate([nn(own_ref[...], mine), nn(sibling_ref[...], theirs)], axis=0)
    coupled = identity(2 * R) + nn(pair.T, inner)
    coupled = 0.5 * (coupled + coupled.T)
    inverse_ref[...] = inverse(coupled, True)


def condense_kernel(
    level, levels, side_ref, own_ref, sibling_ref, inverse_ref, factor_ref, gain_ref, *next_refs
):
    side = side_ref[0]
    mine = factor_ref[0, pl.ds(pl.multiple_of(side * R, R), R), :]
    theirs = factor_ref[0, pl.ds(pl.multiple_of((1 - side) * R, R), R), :]
    pair = jnp.concatenate([mine, theirs], axis=0)
    height = (levels - level) * R
    forcing = nn(jnp.concatenate([own_ref[:height], sibling_ref[:height]], axis=1), pair)
    coefficients = nn(forcing, inverse_ref[...])
    if next_refs:
        head_ref, rest_ref = next_refs
        at, to = height, -R
        for m in range(level + 1, levels):
            low = (m - level - 1) * R
            column = own_ref[at : at + height - low] + sibling_ref[at : at + height - low]
            column = column - nt(coefficients[low:], forcing[low : low + R])
            if m == level + 1:
                head_ref[...] = column[:R]
                rest_ref[0 : height - R, :] = column[R:]
            else:
                rest_ref[to : to + height - low, :] = column
            at += height - low
            to += height - low
    gain_ref[...] = nt(coefficients, mine)


def finish_kernel(levels, rows_ref, factor_ref, *refs):
    gain_refs, out_ref, weights_ref = refs[:levels], refs[levels], refs[levels + 1]
    slots = rows_ref.shape[1]
    tile = min(256, slots)
    steps = slots // tile
    for level in reversed(range(levels)):
        gain = gain_refs[level]
        at = (levels - level - 1) * R
        weight = gain[at : at + R]
        if at > 0:
            weight = weight - nn(weights_ref[:, (level + 1) * R :], gain[0:at])
        weights_ref[:, level * R : (level + 1) * R] = weight
    right = rows_ref[levels * R :, :] - nn(weights_ref[...], rows_ref[: levels * R, :])
    solved = [None] * steps
    for k in reversed(range(steps)):
        ks = slice(k * tile, (k + 1) * tile)
        value = nn(right[:, ks], factor_ref[ks, ks])
        if k < steps - 1:
            later = jnp.concatenate(solved[k + 1 :], axis=1)
            value = value - nn(later, factor_ref[(k + 1) * tile :, ks])
        solved[k] = value
    out_ref[...] = jnp.concatenate(solved, axis=1).T


def swapped(shard, axis, stride):
    return lax.ppermute(shard, axis, [(i, i ^ 1 << stride) for i in range(lax.axis_size(axis))])


def pair_swap(payload, bit_index, sub_bits):
    if bit_index < sub_bits:
        return swapped(payload, "sub", bit_index)
    return swapped(payload, "leaf", bit_index - sub_bits)


def f32(*shape):
    return jax.ShapeDtypeStruct(shape, jnp.float32)


VMEM = pl.BlockSpec(memory_space=pltpu.VMEM)
SMEM = pl.BlockSpec(memory_space=pltpu.SMEM)


def shards(points, order, counts, basis, right_side, coupling):
    slots = points.shape[1]
    levels = basis.shape[1] // R
    columns = (levels + 1) * R
    sub_bits = lax.axis_size("sub").bit_length() - 1
    position = lax.axis_index("leaf") * lax.axis_size("sub") + lax.axis_index("sub")
    head, rest, factor, rows = pl.pallas_call(
        leaf_kernel,
        out_shape=(
            f32(R, R), f32(packed_rows(levels, 0), R), f32(slots, slots), f32(columns, slots),
        ),
        in_specs=[SMEM] + [VMEM] * 4,
        out_specs=(VMEM,) * 4,
        scratch_shapes=[pltpu.VMEM((8, slots), jnp.float32), pltpu.VMEM((columns, slots), jnp.float32)],
        name="leaf",
    )(counts, points, order, basis, right_side)
    gains = []
    for level in range(levels):
        side = (position >> level & 1).astype(jnp.int32).reshape(1)
        other_head = pair_swap(head, level, sub_bits)
        other_rest = pair_swap(rest, level, sub_bits)
        chosen = pl.BlockSpec((1, 2 * R, 2 * R), functools.partial(lambda at, i: (at, 0, 0), level))
        whole = lambda *shape: pl.BlockSpec(shape, lambda i: (0, 0))
        inverted = pl.pallas_call(
            invert_kernel,
            grid=(1,),
            out_shape=f32(2 * R, 2 * R),
            in_specs=[SMEM, whole(R, R), whole(R, R), chosen],
            out_specs=whole(2 * R, 2 * R),
            name=f"invert{level}",
        )(side, head, other_head, coupling)
        shapes = [f32((levels - level) * R, R)]
        if level < levels - 1:
            shapes += [f32(R, R), f32(packed_rows(levels, level + 1), R)]
        outs = pl.pallas_call(
            functools.partial(condense_kernel, level, levels),
            grid=(1,),
            out_shape=shapes,
            in_specs=[SMEM, whole(*rest.shape), whole(*rest.shape), whole(2 * R, 2 * R), chosen],
            out_specs=[whole(*s.shape) for s in shapes],
            name=f"condense{level}",
        )(side, rest, other_rest, inverted, coupling)
        gains.append(outs[0])
        if level < levels - 1:
            head, rest = outs[1:]
    return pl.pallas_call(
        functools.partial(finish_kernel, levels),
        out_shape=f32(slots, R),
        in_specs=[VMEM] * (2 + levels),
        out_specs=VMEM,
        scratch_shapes=[pltpu.VMEM((R, levels * R), jnp.float32)],
        name="finish",
    )(rows, factor, *gains)


def solution(mesh):
    placed = (
        P(None, ("leaf", "sub")),
        P(("leaf", "sub"), None),
        P(("leaf", "sub")),
        P(("leaf", "sub"), None),
        P(("leaf", "sub"), None),
        P(),
    )
    return jax.shard_map(
        shards, mesh=mesh, in_specs=placed, out_specs=P(("leaf", "sub"), None), check_vma=False
    )
```

```python
import functools
import math

import jax
import jax.numpy as jnp
from jax import lax
from jax.experimental import pallas as pl
from jax.experimental.pallas import tpu as pltpu
from jax.sharding import PartitionSpec as P


R = 128
GAMMA_RATE = 2.0
NUGGET_VALUE = 1.0
HIGH = lax.Precision.HIGH
HIGHEST = lax.Precision.HIGHEST


def nn(a, b, precision=HIGH):
    return lax.dot_general(
        a, b, (((1,), (0,)), ((), ())), precision=precision, preferred_element_type=jnp.float32
    )


def nt(a, b, precision=HIGH):
    return lax.dot_general(
        a, b, (((1,), (1,)), ((), ())), precision=precision, preferred_element_type=jnp.float32
    )


def identity(size):
    row = lax.broadcasted_iota(jnp.int32, (size, size), 0)
    col = lax.broadcasted_iota(jnp.int32, (size, size), 1)
    return (row == col).astype(jnp.float32)


def inverse(matrix, refine):
    size = matrix.shape[0]
    eye = identity(size)
    low = 1.0 / jnp.max(jnp.sum(jnp.abs(matrix), axis=0))

    def step(carry):
        low, x, z = carry
        scale = 4.0 / ((1.0 + low) * (1.0 + low))
        shift = 1.0 + low
        return (
            low * scale,
            scale * (shift * x - nn(x, z)),
            scale * (shift * z - nn(z, z)),
        )

    _, x, _ = lax.while_loop(
        lambda carry: carry[0] < 1.0 - 6e-7, step, (low, eye * low, matrix * low)
    )
    if refine:
        x = x + nn(x, eye - nn(matrix, x, HIGHEST))
    return x


def leaf_kernel(
    count_ref, points_ref, order_ref, basis_ref, rhs_ref,
    head_ref, near_rows_ref, far_rows_ref, factor_ref, rows_ref,
    near_points_ref, near_order_ref, coords_ref, weighted_ref, near_basis_ref, near_rhs_ref, sems,
):
    fetches = [
        pltpu.make_async_copy(points_ref, near_points_ref, sems.at[0]),
        pltpu.make_async_copy(order_ref, near_order_ref, sems.at[1]),
        pltpu.make_async_copy(basis_ref, near_basis_ref, sems.at[2]),
        pltpu.make_async_copy(rhs_ref, near_rhs_ref, sems.at[3]),
    ]
    for fetch in fetches:
        fetch.start()
    slots = points_ref.shape[1]
    levels = basis_ref.shape[1] // R
    blocks = levels + 1
    tile = min(256, slots)
    count = count_ref[0]
    coords_ref[...] = jnp.zeros_like(coords_ref)
    fetches[0].wait()
    coords_ref[0:3, :] = near_points_ref[...]
    coords = coords_ref[...]
    first = coords.astype(jnp.bfloat16).astype(jnp.float32)
    second = (coords - first).astype(jnp.bfloat16).astype(jnp.float32)
    third = coords - first - second
    parts = jnp.concatenate([first, second, third], axis=0).astype(jnp.bfloat16)
    source = lax.broadcasted_iota(jnp.int32, (slots, slots), 0)
    fetches[1].wait()
    chosen = jnp.where(source == near_order_ref[...], 1.0, 0.0).astype(jnp.bfloat16)
    moved = jnp.dot(parts, chosen, preferred_element_type=jnp.float32)
    across = moved[0:8] + moved[8:16] + moved[16:24]
    down = across.T
    live_across = (lax.broadcasted_iota(jnp.int32, (1, slots), 1) < count).astype(jnp.float32)
    live_down = (lax.broadcasted_iota(jnp.int32, (slots, 1), 0) < count).astype(jnp.float32)
    steps = slots // tile
    for j in range(steps):
        js = slice(j * tile, (j + 1) * tile)
        for i in range(j, steps):
            rs = slice(i * tile, (i + 1) * tile)
            total = None
            for axis in range(3):
                offset = down[rs, axis : axis + 1] - across[axis : axis + 1, js]
                square = offset * offset
                total = square if total is None else total + square
            value = jnp.exp2(total * (-GAMMA_RATE * math.log2(math.e)))
            value = value * live_down[rs] * live_across[:, js]
            if i == j:
                value = value + NUGGET_VALUE * identity(tile)
            factor_ref[rs, js] = value
    for fetch in fetches[2:]:
        fetch.wait()
    for block in range(blocks):
        if block < levels:
            piece = near_basis_ref[:, block * R : (block + 1) * R]
        else:
            piece = near_rhs_ref[...]
        rows_ref[block * R : (block + 1) * R, :] = piece.T * live_across
    for k in range(steps):
        ks = slice(k * tile, (k + 1) * tile)
        x = inverse(factor_ref[ks, ks], False)
        factor_ref[ks, ks] = x
        own = rows_ref[:, ks]
        if k < steps - 1:
            panel = factor_ref[(k + 1) * tile :, ks]
            lower = nn(panel, x)
            factor_ref[(k + 1) * tile :, ks] = lower
            for j in range(k + 1, steps):
                js = slice(j * tile, (j + 1) * tile)
                at = (j - k - 1) * tile
                factor_ref[j * tile :, js] -= nt(lower[at:], panel[at : at + tile])
            rows_ref[:, (k + 1) * tile :] -= nt(own, lower)
        weighted_ref[:, ks] = nn(own, x)
    for m in range(levels):
        column = nt(weighted_ref[m * R :, :], rows_ref[m * R : (m + 1) * R, :])
        if m == 0:
            head_ref[...] = column[:R]
        for c in range(max(m, 1), blocks):
            piece = column[(c - m) * R : (c - m + 1) * R]
            if c == 1:
                near_rows_ref[:, m * R : (m + 1) * R] = piece
            else:
                at = (row_start(levels, 0, 2, c) + m) * R
                far_rows_ref[:, at : at + R] = piece


def row_blocks(levels, level, row):
    return min(row, levels - 1) - level + 1


def row_start(levels, level, first, row):
    return sum(row_blocks(levels, level, c) for c in range(first, row))


def side_of(level):
    sub_bits = lax.axis_size("sub").bit_length() - 1
    if level < sub_bits:
        return lax.axis_index("sub") >> level & 1
    return lax.axis_index("leaf") >> (level - sub_bits) & 1


def invert_kernel(level, own_ref, sibling_ref, factor_ref, after_ref, inverse_ref, token_ref):
    side = side_of(level)
    mine = factor_ref[level, pl.ds(pl.multiple_of(side * R, R), R), :]
    theirs = factor_ref[level, pl.ds(pl.multiple_of((1 - side) * R, R), R), :]
    pair = jnp.concatenate([mine, theirs], axis=0)
    inner = jnp.concatenate([nn(own_ref[...], mine), nn(sibling_ref[...], theirs)], axis=0)
    coupled = identity(2 * R) + nn(pair.T, inner)
    coupled = 0.5 * (coupled + coupled.T)
    inverse_ref[...] = inverse(coupled, True)
    token_ref[...] = jnp.zeros_like(token_ref)


def condense_kernel(level, levels, group, *refs):
    own_ref, sibling_ref, inverse_ref, factor_ref = refs[:4]
    known = group[0] - level - 1
    forcing_refs, refs = refs[4 : 4 + known], refs[4 + known :]
    refs = refs[1:]
    passed = [row for row in group if row > level + 1 or level < levels - 1]
    next_refs, refs = refs[: len(passed)], refs[len(passed) :]
    new_forcing_refs, gain_refs, token_ref = refs[: len(group)], refs[len(group) : -1], refs[-1]
    side = side_of(level)
    mine = factor_ref[level, pl.ds(pl.multiple_of(side * R, R), R), :]
    theirs = factor_ref[level, pl.ds(pl.multiple_of((1 - side) * R, R), R), :]
    pair = jnp.concatenate([mine, theirs], axis=0)
    starts = [row_start(levels, level, group[0], row) * R for row in group]
    own_side = jnp.concatenate([own_ref[:, at : at + R] for at in starts], axis=0)
    other_side = jnp.concatenate([sibling_ref[:, at : at + R] for at in starts], axis=0)
    forcing = nn(jnp.concatenate([own_side, other_side], axis=1), pair)
    coefficients = nn(forcing, inverse_ref[...])
    gains = nt(coefficients, mine)
    every = [ref[...] for ref in forcing_refs]
    for index, row in enumerate(group):
        piece = forcing[index * R : (index + 1) * R]
        new_forcing_refs[index][...] = piece
        gain_refs[index][...] = gains[index * R : (index + 1) * R]
        every.append(piece)
    for index, row in enumerate(group):
        width = (row_blocks(levels, level, row) - 1) * R
        if width == 0:
            continue
        at = starts[index] + R
        total = own_ref[:, at : at + width] + sibling_ref[:, at : at + width]
        against = jnp.concatenate(every[: width // R], axis=0)
        part = coefficients[index * R : (index + 1) * R]
        next_refs[index][...] = total - nt(part, against)
    token_ref[...] = jnp.zeros_like(token_ref)


def finish_kernel(levels, rows_ref, factor_ref, *refs):
    out_ref, weights_ref = refs[-2:]
    slots = rows_ref.shape[1]
    tile = min(256, slots)
    steps = slots // tile
    end = len(refs) - 2
    for level in reversed(range(levels)):
        start = end - (levels - level)
        weight = refs[end - 1][...]
        if level < levels - 1:
            gain = jnp.concatenate([ref[...] for ref in refs[start : end - 1]], axis=0)
            weight = weight - nn(weights_ref[:, (level + 1) * R :], gain)
        weights_ref[:, level * R : (level + 1) * R] = weight
        end = start
    right = rows_ref[levels * R :, :] - nn(weights_ref[...], rows_ref[: levels * R, :])
    solved = [None] * steps
    for k in reversed(range(steps)):
        ks = slice(k * tile, (k + 1) * tile)
        value = nn(right[:, ks], factor_ref[ks, ks])
        if k < steps - 1:
            later = jnp.concatenate(solved[k + 1 :], axis=1)
            value = value - nn(later, factor_ref[(k + 1) * tile :, ks])
        solved[k] = value
    out_ref[...] = jnp.concatenate(solved, axis=1).T


def swapped(shard, axis, stride):
    return lax.ppermute(shard, axis, [(i, i ^ 1 << stride) for i in range(lax.axis_size(axis))])


def pair_swap(payload, bit_index, sub_bits):
    if bit_index < sub_bits:
        return swapped(payload, "sub", bit_index)
    return swapped(payload, "leaf", bit_index - sub_bits)


def f32(*shape):
    return jax.ShapeDtypeStruct(shape, jnp.float32)


def near(*shape):
    return pltpu.VMEM(shape, jnp.float32)


def far_away(value):
    return pltpu.with_memory_space_constraint(value, pltpu.HBM)


def hold(value):
    return pltpu.with_memory_space_constraint(value, pltpu.VMEM)


VMEM = pl.BlockSpec(memory_space=pltpu.VMEM)
HBM = pl.BlockSpec(memory_space=pltpu.HBM)
SMEM = pl.BlockSpec(memory_space=pltpu.SMEM)
LIMIT = pltpu.CompilerParams(vmem_limit_bytes=12 << 20)
LEAF_LIMIT = pltpu.CompilerParams(vmem_limit_bytes=24 << 20)


def schedule(levels):
    others = tuple(range(2, levels + 1))
    plan = [("invert", 0), ("condense", 0, (1,)), ("condense", 0, others)]
    for level in range(1, levels):
        plan += [("invert", level), ("condense", level, (level + 1,))]
        for at in range(1, level + 1):
            if at > 1 and level + 3 <= levels:
                plan.append(("condense", at - 1, (level + 3,)))
            if level + 2 <= levels:
                plan.append(("condense", at, (level + 2,)))
    return list(dict.fromkeys(plan))


def shards(points, order, counts, basis, right_side, coupling):
    slots = points.shape[1]
    levels = basis.shape[1] // R
    columns = (levels + 1) * R
    sub_bits = lax.axis_size("sub").bit_length() - 1
    coupling = hold(coupling)
    token = near(8, R)
    head, close, far, factor, rows = pl.pallas_call(
        leaf_kernel,
        out_shape=(
            near(R, R), near(R, 2 * R), near(R, row_start(levels, 0, 2, levels + 1) * R),
            near(slots, slots), near(columns, slots),
        ),
        in_specs=[SMEM] + [HBM] * 4,
        out_specs=(VMEM,) * 5,
        scratch_shapes=[
            near(*points.shape), pltpu.VMEM(order.shape, jnp.int32), near(8, slots),
            near(columns, slots), near(*basis.shape), near(*right_side.shape),
            pltpu.SemaphoreType.DMA((4,)),
        ],
        compiler_params=LEAF_LIMIT,
        name="leaf",
    )(counts, *[far_away(x) for x in (points, order, basis, right_side)])

    gains = {}
    forcing = {}
    sent = {}
    inverted = {}
    chain = [jnp.zeros((8, R), jnp.float32)]

    def send(level, group, value):
        sent[level, group] = (value, hold(pair_swap(value, level, sub_bits)))

    def invert(level):
        inverted[level], chain[0] = pl.pallas_call(
            functools.partial(invert_kernel, level),
            out_shape=(near(2 * R, 2 * R), token),
            in_specs=[VMEM] * 4,
            out_specs=[VMEM] * 2,
            compiler_params=LIMIT,
        )(*sent[level, (level,)], coupling, hold(chain[0]))

    def condense(level, group):
        known = range(level + 1, group[0])
        widths = [row_blocks(levels, level, row) - 1 for row in group]
        shapes = [near(R, width * R) for width in widths if width > 0]
        passed = len(shapes)
        shapes += [near(R, 2 * R)] * len(group) + [near(R, R)] * len(group) + [token]
        outs = pl.pallas_call(
            functools.partial(condense_kernel, level, levels, group),
            out_shape=shapes,
            in_specs=[VMEM] * (5 + len(known)),
            out_specs=[VMEM] * len(shapes),
            compiler_params=LIMIT,
        )(
            *sent[level, group], inverted[level], coupling,
            *[forcing[level, row] for row in known], hold(chain[0]),
        )
        chain[0] = outs[-1]
        for index, row in enumerate(group):
            forcing[level, row] = outs[passed + index]
            gains[level, row] = outs[passed + len(group) + index]
        return [(level + 1, (group[index],), outs[index]) for index in range(passed)]

    others = tuple(range(2, levels + 1))
    send(0, (0,), head)
    send(0, (1,), close)
    send(0, others, far)
    for step in schedule(levels):
        if step[0] == "invert":
            invert(step[1])
        else:
            made = condense(*step[1:])
        if step[0] == "condense":
            for one in made:
                send(*one)
    return pl.pallas_call(
        functools.partial(finish_kernel, levels),
        out_shape=f32(slots, R),
        in_specs=[VMEM] * (2 + len(gains)),
        out_specs=VMEM,
        scratch_shapes=[pltpu.VMEM((R, levels * R), jnp.float32)],
        compiler_params=LIMIT,
        name="finish",
    )(rows, factor, *[gains[key] for key in sorted(gains)])


def solution(mesh):
    placed = (
        P(None, ("leaf", "sub")),
        P(("leaf", "sub"), None),
        P(("leaf", "sub")),
        P(("leaf", "sub"), None),
        P(("leaf", "sub"), None),
        P(),
    )

    def step(points, order, counts, basis, right_side, coupling):
        whole = jax.shard_map(
            shards, mesh=mesh, in_specs=placed, out_specs=P(("leaf", "sub"), None), check_vma=False
        )
        return whole(points, order, counts, basis, right_side, coupling)

    return step
```

```python
import functools
import math

import jax
import jax.numpy as jnp
from jax import lax
from jax.experimental import pallas as pl
from jax.experimental.pallas import tpu as pltpu
from jax.sharding import PartitionSpec as P


R = 128
GAMMA_RATE = 2.0
NUGGET_VALUE = 1.0
HIGH = lax.Precision.HIGH
HIGHEST = lax.Precision.HIGHEST


def nn(a, b, precision=HIGH):
    return lax.dot_general(
        a, b, (((1,), (0,)), ((), ())), precision=precision, preferred_element_type=jnp.float32
    )


def nt(a, b, precision=HIGH):
    return lax.dot_general(
        a, b, (((1,), (1,)), ((), ())), precision=precision, preferred_element_type=jnp.float32
    )


def identity(size):
    row = lax.broadcasted_iota(jnp.int32, (size, size), 0)
    col = lax.broadcasted_iota(jnp.int32, (size, size), 1)
    return (row == col).astype(jnp.float32)


def inverse(matrix, refine):
    size = matrix.shape[0]
    eye = identity(size)
    low = 1.0 / jnp.max(jnp.sum(jnp.abs(matrix), axis=0))
    slack = 1e-3 if refine else 3e-6
    z = matrix * low
    scale = 4.0 / ((1.0 + low) * (1.0 + low))
    shift = 1.0 + low
    first = (low * scale, (scale * low) * (shift * eye - z), scale * (shift * z - nn(z, z)))

    def step(carry):
        low, x, z = carry
        scale = 4.0 / ((1.0 + low) * (1.0 + low))
        shift = 1.0 + low
        return (
            low * scale,
            scale * (shift * x - nn(x, z)),
            scale * (shift * z - nn(z, z)),
        )

    _, x, _ = lax.while_loop(lambda carry: carry[0] < 1.0 - slack, step, first)
    if refine:
        x = x + nn(x, eye - nn(matrix, x, HIGHEST))
    return x


def leaf_kernel(
    count_ref, points_ref, order_ref, basis_ref, rhs_ref,
    head_ref, near_rows_ref, far_rows_ref, factor_ref, rows_ref,
    near_points_ref, near_order_ref, coords_ref, weighted_ref, near_basis_ref, near_rhs_ref, sems,
):
    fetches = [
        pltpu.make_async_copy(points_ref, near_points_ref, sems.at[0]),
        pltpu.make_async_copy(order_ref, near_order_ref, sems.at[1]),
        pltpu.make_async_copy(basis_ref, near_basis_ref, sems.at[2]),
        pltpu.make_async_copy(rhs_ref, near_rhs_ref, sems.at[3]),
    ]
    for fetch in fetches:
        fetch.start()
    slots = points_ref.shape[1]
    levels = basis_ref.shape[1] // R
    blocks = levels + 1
    tile = min(256, slots)
    count = count_ref[0]
    coords_ref[...] = jnp.zeros_like(coords_ref)
    fetches[0].wait()
    coords_ref[0:3, :] = near_points_ref[...]
    coords = coords_ref[...]
    first = coords.astype(jnp.bfloat16).astype(jnp.float32)
    second = (coords - first).astype(jnp.bfloat16).astype(jnp.float32)
    third = coords - first - second
    parts = jnp.concatenate([first, second, third], axis=0).astype(jnp.bfloat16)
    source = lax.broadcasted_iota(jnp.int32, (slots, slots), 0)
    fetches[1].wait()
    chosen = jnp.where(source == near_order_ref[...], 1.0, 0.0).astype(jnp.bfloat16)
    moved = jnp.dot(parts, chosen, preferred_element_type=jnp.float32)
    across = moved[0:8] + moved[8:16] + moved[16:24]
    down = across.T
    live_across = (lax.broadcasted_iota(jnp.int32, (1, slots), 1) < count).astype(jnp.float32)
    live_down = (lax.broadcasted_iota(jnp.int32, (slots, 1), 0) < count).astype(jnp.float32)
    steps = slots // tile
    for j in range(steps):
        js = slice(j * tile, (j + 1) * tile)
        for i in range(j, steps):
            rs = slice(i * tile, (i + 1) * tile)
            total = None
            for axis in range(3):
                offset = down[rs, axis : axis + 1] - across[axis : axis + 1, js]
                square = offset * offset
                total = square if total is None else total + square
            value = jnp.exp2(total * (-GAMMA_RATE * math.log2(math.e)))
            value = value * live_down[rs] * live_across[:, js]
            if i == j:
                value = value + NUGGET_VALUE * identity(tile)
            factor_ref[rs, js] = value
    for fetch in fetches[2:]:
        fetch.wait()
    for block in range(blocks):
        if block < levels:
            piece = near_basis_ref[:, block * R : (block + 1) * R]
        else:
            piece = near_rhs_ref[...]
        rows_ref[block * R : (block + 1) * R, :] = piece.T * live_across
    for k in range(steps):
        ks = slice(k * tile, (k + 1) * tile)
        x = inverse(factor_ref[ks, ks], False)
        factor_ref[ks, ks] = x
        own = rows_ref[:, ks]
        if k < steps - 1:
            panel = factor_ref[(k + 1) * tile :, ks]
            lower = nn(panel, x)
            factor_ref[(k + 1) * tile :, ks] = lower
            for j in range(k + 1, steps):
                js = slice(j * tile, (j + 1) * tile)
                at = (j - k - 1) * tile
                factor_ref[j * tile :, js] -= nt(lower[at:], panel[at : at + tile])
            rows_ref[:, (k + 1) * tile :] -= nt(own, lower)
        weighted_ref[:, ks] = nn(own, x)
    for pair in range(0, levels, 2):
        wide = range(pair, min(pair + 2, levels))
        columns = nt(weighted_ref[pair * R :, :], rows_ref[pair * R : (wide[-1] + 1) * R, :])
        for m in wide:
            if m == 0:
                head_ref[...] = columns[:R, :R]
            for c in range(max(m, 1), blocks):
                piece = columns[(c - pair) * R : (c - pair + 1) * R, (m - pair) * R : (m - pair + 1) * R]
                if c == 1:
                    near_rows_ref[:, m * R : (m + 1) * R] = piece
                else:
                    at = (row_start(levels, 0, 2, c) + m) * R
                    far_rows_ref[:, at : at + R] = piece


def row_blocks(levels, level, row):
    return min(row, levels - 1) - level + 1


def row_start(levels, level, first, row):
    return sum(row_blocks(levels, level, c) for c in range(first, row))


def side_of(level):
    sub_bits = lax.axis_size("sub").bit_length() - 1
    if level < sub_bits:
        return lax.axis_index("sub") >> level & 1
    return lax.axis_index("leaf") >> (level - sub_bits) & 1


def invert_kernel(level, levels, own_ref, *refs):
    sibling_refs, (factor_ref, _, inverse_ref, token_ref) = refs[:-4], refs[-4:]
    sibling = sibling_refs[0][...]
    if len(sibling_refs) > 1:
        sibling = chosen_row(levels, level, sibling, sibling_refs[1][...])
    side = side_of(level)
    mine = factor_ref[level, pl.ds(pl.multiple_of(side * R, R), R), :]
    theirs = factor_ref[level, pl.ds(pl.multiple_of((1 - side) * R, R), R), :]
    pair = jnp.concatenate([mine, theirs], axis=0)
    inner = jnp.concatenate([nn(own_ref[...], mine), nn(sibling, theirs)], axis=0)
    coupled = identity(2 * R) + nn(pair.T, inner)
    coupled = 0.5 * (coupled + coupled.T)
    inverse_ref[...] = inverse(coupled, True)
    token_ref[...] = jnp.zeros_like(token_ref)


def groups_of(levels, level):
    if level == 0:
        return [(1,), tuple(range(2, levels + 1))]
    if level == levels - 1:
        return [(levels,)]
    return [(row,) for row in range(level + 1, levels - 1)] + [(levels - 1, levels)]


def is_split(levels, level, group):
    return level > 0 and (len(group) == 2 or level == levels - 1)


def has_portion(levels, level, group):
    return is_split(levels, level, group) and group[-1] == levels


def chosen_row(levels, row, direct, passed_on):
    return jnp.where(side_of(0) == row - (levels - 1), direct, passed_on)


def width_of(levels, level, group):
    return row_start(levels, level, group[0], group[-1] + 1) * R


def next_groups(levels, level, group):
    found = []
    if group[0] == level + 1 < levels:
        found.append((level + 1,))
    if level < levels - 1:
        found += [one for one in groups_of(levels, level + 1) if set(one) <= set(group)]
    return found


def condense_kernel(level, levels, group, *refs):
    refs = list(refs)
    take = lambda count: [refs.pop(0) for _ in range(count)]
    (own_ref,) = take(1)
    sibling_refs = take(2 if is_split(levels, level, group) else 1)
    inverse_ref, factor_ref = take(2)
    forcing_refs = take(group[0] - level - 1)
    take(1)
    after = next_groups(levels, level, group)
    targets = [take(2 if has_portion(levels, level + 1, one) else 1) for one in after]
    new_forcing_refs, gain_refs = take(len(group)), take(len(group))
    (token_ref,) = refs
    side = side_of(level)
    mine = factor_ref[level, pl.ds(pl.multiple_of(side * R, R), R), :]
    theirs = factor_ref[level, pl.ds(pl.multiple_of((1 - side) * R, R), R), :]
    pair = jnp.concatenate([mine, theirs], axis=0)
    own, sibling = {}, {}
    for row in group:
        at = row_start(levels, level, group[0], row) * R
        width = row_blocks(levels, level, row) * R
        own[row] = own_ref[:, at : at + width]
        if is_split(levels, level, group):
            sibling[row] = chosen_row(levels, row, sibling_refs[0][...], sibling_refs[1][...])
        else:
            sibling[row] = sibling_refs[0][:, at : at + width]
    own_side = jnp.concatenate([own[row][:, :R] for row in group], axis=0)
    other_side = jnp.concatenate([sibling[row][:, :R] for row in group], axis=0)
    forcing = nn(jnp.concatenate([own_side, other_side], axis=1), pair)
    coefficients = nn(forcing, inverse_ref[...])
    every = [ref[...] for ref in forcing_refs]
    for index, row in enumerate(group):
        piece = forcing[index * R : (index + 1) * R]
        new_forcing_refs[index][...] = piece
        every.append(piece)
    reduced = {}
    for index, row in enumerate(group):
        width = row_blocks(levels, level, row) - 1
        if width > 0:
            total = own[row][:, R:] + sibling[row][:, R:]
            part = coefficients[index * R : (index + 1) * R]
            reduced[row] = total - nt(part, jnp.concatenate(every[:width], axis=0))
    for one, target in zip(after, targets):
        for row in one:
            at = 0 if len(one) == 1 else row_start(levels, level + 1, one[0], row) * R
            target[0][:, at : at + reduced[row].shape[1]] = reduced[row]
        if has_portion(levels, level + 1, one):
            target[1][...] = chosen_row(levels, levels, reduced[levels], reduced[levels - 1])
    gains = nt(coefficients, mine)
    for index in range(len(group)):
        gain_refs[index][...] = gains[index * R : (index + 1) * R]
    token_ref[...] = jnp.zeros_like(token_ref)


def finish_kernel(levels, rows_ref, factor_ref, *refs):
    out_ref, weights_ref = refs[-2:]
    slots = rows_ref.shape[1]
    tile = min(256, slots)
    steps = slots // tile
    end = len(refs) - 2
    for level in reversed(range(levels)):
        start = end - (levels - level)
        weight = refs[end - 1][...]
        if level < levels - 1:
            gain = jnp.concatenate([ref[...] for ref in refs[start : end - 1]], axis=0)
            weight = weight - nn(weights_ref[:, (level + 1) * R :], gain)
        weights_ref[:, level * R : (level + 1) * R] = weight
        end = start
    right = rows_ref[levels * R :, :] - nn(weights_ref[...], rows_ref[: levels * R, :])
    solved = [None] * steps
    for k in reversed(range(steps)):
        ks = slice(k * tile, (k + 1) * tile)
        value = nn(right[:, ks], factor_ref[ks, ks])
        if k < steps - 1:
            later = jnp.concatenate(solved[k + 1 :], axis=1)
            value = value - nn(later, factor_ref[(k + 1) * tile :, ks])
        solved[k] = value
    out_ref[...] = jnp.concatenate(solved, axis=1).T


def swapped(shard, axis, stride):
    return lax.ppermute(shard, axis, [(i, i ^ 1 << stride) for i in range(lax.axis_size(axis))])


def pair_swap(payload, bit_index, sub_bits):
    if bit_index < sub_bits:
        return swapped(payload, "sub", bit_index)
    return swapped(payload, "leaf", bit_index - sub_bits)


def f32(*shape):
    return jax.ShapeDtypeStruct(shape, jnp.float32)


def near(*shape):
    return pltpu.VMEM(shape, jnp.float32)


def far_away(value):
    return pltpu.with_memory_space_constraint(value, pltpu.HBM)


def hold(value):
    return pltpu.with_memory_space_constraint(value, pltpu.VMEM)


VMEM = pl.BlockSpec(memory_space=pltpu.VMEM)
HBM = pl.BlockSpec(memory_space=pltpu.HBM)
SMEM = pl.BlockSpec(memory_space=pltpu.SMEM)
LIMIT = pltpu.CompilerParams(vmem_limit_bytes=12 << 20)
LEAF_LIMIT = pltpu.CompilerParams(vmem_limit_bytes=24 << 20)


def schedule(levels):
    first, rest = groups_of(levels, 0)
    plan = [("invert", 0), ("condense", 0, first), ("condense", 0, rest)]
    for level in range(1, levels):
        plan.append(("invert", level))
        plan += [("condense", level, rows) for rows in groups_of(levels, level)]
    return plan


def shards(points, order, counts, basis, right_side, coupling):
    slots = points.shape[1]
    levels = basis.shape[1] // R
    columns = (levels + 1) * R
    sub_bits = lax.axis_size("sub").bit_length() - 1
    coupling = hold(coupling)
    token = near(8, R)
    head, close, far, factor, rows = pl.pallas_call(
        leaf_kernel,
        out_shape=(
            near(R, R), near(R, 2 * R), near(R, row_start(levels, 0, 2, levels + 1) * R),
            near(slots, slots), near(columns, slots),
        ),
        in_specs=[SMEM] + [HBM] * 4,
        out_specs=(VMEM,) * 5,
        scratch_shapes=[
            near(*points.shape), pltpu.VMEM(order.shape, jnp.int32), near(8, slots),
            near(columns, slots), near(*basis.shape), near(*right_side.shape),
            pltpu.SemaphoreType.DMA((4,)),
        ],
        compiler_params=LEAF_LIMIT,
        name="leaf",
    )(counts, *[far_away(x) for x in (points, order, basis, right_side)])

    gains = {}
    forcing = {}
    sent = {}
    waiting = {}
    inverted = {}
    chain = [jnp.zeros((8, R), jnp.float32)]

    def send(level, group, own, portion=None):
        if portion is None and is_split(levels, level, group):
            waiting[level] = own
            return
        arrived = [hold(pair_swap(own if portion is None else portion, level, sub_bits))]
        if portion is not None:
            arrived.append(hold(pair_swap(arrived[0], 0, sub_bits)))
        sent[level, group] = (own, *arrived)
        if level in waiting:
            sent[level, (level,)] = (waiting[level], *arrived)

    def invert(level):
        operands = [*sent[level, (level,)], coupling, hold(chain[0])]
        inverted[level], chain[0] = pl.pallas_call(
            functools.partial(invert_kernel, level, levels),
            out_shape=(near(2 * R, 2 * R), token),
            in_specs=[VMEM] * len(operands),
            out_specs=[VMEM] * 2,
            compiler_params=LIMIT,
        )(*operands)

    def condense(level, group):
        known = range(level + 1, group[0])
        after = next_groups(levels, level, group)
        shapes = []
        for one in after:
            width = R if one == (level + 1,) else width_of(levels, level + 1, one)
            shapes.append(near(R, width))
            if has_portion(levels, level + 1, one):
                shapes.append(near(R, width // len(one)))
        passed = len(shapes)
        shapes += [near(R, 2 * R)] * len(group) + [near(R, R)] * len(group) + [token]
        operands = [
            *sent[level, group], inverted[level], coupling,
            *[forcing[level, row] for row in known], hold(chain[0]),
        ]
        outs = pl.pallas_call(
            functools.partial(condense_kernel, level, levels, group),
            out_shape=shapes,
            in_specs=[VMEM] * len(operands),
            out_specs=[VMEM] * len(shapes),
            compiler_params=LIMIT,
        )(*operands)
        chain[0] = outs[-1]
        for index, row in enumerate(group):
            forcing[level, row] = outs[passed + index]
            gains[level, row] = outs[passed + len(group) + index]
        made = list(outs[:passed])
        return [
            (level + 1, one, *[made.pop(0) for _ in range(2 if has_portion(levels, level + 1, one) else 1)])
            for one in after
        ]

    others = tuple(range(2, levels + 1))
    send(0, (0,), head)
    send(0, (1,), close)
    send(0, others, far)
    for step in schedule(levels):
        if step[0] == "invert":
            invert(step[1])
        else:
            made = condense(*step[1:])
        if step[0] == "condense":
            for one in made:
                send(*one)
    return pl.pallas_call(
        functools.partial(finish_kernel, levels),
        out_shape=f32(slots, R),
        in_specs=[VMEM] * (2 + len(gains)),
        out_specs=VMEM,
        scratch_shapes=[pltpu.VMEM((R, levels * R), jnp.float32)],
        compiler_params=LIMIT,
        name="finish",
    )(rows, factor, *[gains[key] for key in sorted(gains)])


def solution(mesh):
    placed = (
        P(None, ("leaf", "sub")),
        P(("leaf", "sub"), None),
        P(("leaf", "sub")),
        P(("leaf", "sub"), None),
        P(("leaf", "sub"), None),
        P(),
    )

    def step(points, order, counts, basis, right_side, coupling):
        whole = jax.shard_map(
            shards, mesh=mesh, in_specs=placed, out_specs=P(("leaf", "sub"), None), check_vma=False
        )
        return whole(points, order, counts, basis, right_side, coupling)

    return step
```
